32 devices in a mesh: member: 8 (over z, x), tile: 4 (over y, core).
Axes of the slice: x: 2, y: 2, z: 4, core: 2. Of those that a mesh axis runs over, the one named last changes fastest.
Arguments:
- ensemble: bfloat16 [256, 128, 320], P('member', 'tile'), may hold values from -6 to 6
- departures: bfloat16 [128, 128, 256], P(('tile', 'member')), may hold values from -6 to 6
- innovations: float32 [128, 128], P(('tile', 'member')), may hold values from -12 to 12
- precision: float32 [128, 128], P(('tile', 'member')), may hold values from 0.2 to 5
- obs_count: int32 [128], P(('tile', 'member')), may hold values from 16 to 128
- tile_counts: int32 [4], replicated, may hold values from 0 to 32, as said below
Outputs:
- analysis: bfloat16 [256, 128, 320], P('member', 'tile')
The draws below stay inside these ranges and needn't reach their ends.
Inputs may be any that keep to these rules, and one draw needn't show every extreme that they name: `tile_counts`: each count is a multiple of 8; all counts sum to 64, and for every tile t the counts of tiles 0 to t - 1 sum to t * 8 * 2 plus or minus at most 8.
All inputs are finite; a program needn't handle non-finite values.
Results may differ from the reference program's by a relative error of at most 0.0049.
Values may be sent and summed in bfloat16 or wider, within the bound.
A program may use at most 64 MiB of HBM per device.

```python
import math
import jax
import jax.numpy as jnp
from jax import lax

K = 256
V = 320
P_SIZE = 128
WORK = 2
ITERS = 6
LOC = 4
COLS = 128
N_MEMBER = 8
N_TILE = 4


def draw_tile_counts(key, part):
    reach = WORK // 2
    walk_key, summit_key = jax.random.split(jax.random.fold_in(key, 11))
    offsets = jax.random.randint(walk_key, (N_TILE + 1,), -reach, reach + 1)
    borders = jnp.arange(N_TILE + 1)
    offsets = jnp.where((borders == 0) | (borders == N_TILE), 0, offsets)
    summit = jax.random.randint(summit_key, (), 1, N_TILE - 1)
    offsets = jnp.where(borders == summit, -reach, offsets)
    offsets = jnp.where(borders == summit + 1, reach, offsets)
    per_tile = WORK + offsets[1:] - offsets[:-1]
    return (per_tile * N_MEMBER).astype(jnp.int32)


def plant(drawn, own_key, low, high):
    dims = drawn.shape
    index_at = [jax.random.randint(jax.random.fold_in(own_key, axis), (), 0, dims[axis]) for axis in range(len(dims))]
    drawn = drawn.at[tuple(index_at)].set(low)
    longest = dims.index(max(dims))
    index_at[longest] = (index_at[longest] + 1) % dims[longest]
    return drawn.at[tuple(index_at)].set(high)


def levels(own_key, shape, cuts, least, top_value):
    level, own = 1.0, jax.random.fold_in(own_key, 6)
    for position, shards_of in cuts:
        steps = jnp.exp(jax.random.uniform(jax.random.fold_in(own, position), (shards_of,), jnp.float32, least / len(cuts), top_value / len(cuts)))
        level = level * jnp.repeat(steps, shape[position] // shards_of).reshape([-1 if axis == position else 1 for axis in range(len(shape))])
    return level


def gaussian(rng, shape, width, bound, cuts=(), held_as=jnp.bfloat16):
    factor_of = levels(rng, shape, cuts, -0.22, 0.18) if cuts else 1.0
    drawn = jax.random.normal(rng, shape, jnp.float32) * width * factor_of
    return jnp.minimum(jnp.maximum(drawn, -bound), bound).astype(held_as)


def setup_inputs(seed: int = 0) -> dict:
    streams_of = jax.random.split(jax.random.key(seed), 7)
    return {
        "ensemble": gaussian(streams_of[0], (K, COLS, V), 1.0, 6.0, ((0, 8), (1, 4))),
        "departures": gaussian(streams_of[1], (COLS, P_SIZE, K), 1.0, 6.0, ((0, 32),)),
        "innovations": gaussian(streams_of[2], (COLS, P_SIZE), 2.0, 12.0, ((0, 32),), jnp.float32),
        "precision": jnp.clip(jnp.exp(math.log(5.0) - 3.218876 * jax.random.uniform(streams_of[3], (COLS, P_SIZE), jnp.float32) ** levels(streams_of[3], (COLS, P_SIZE), ((0, 32),), -0.2, 0.2)), 0.2, 5.0),
        "obs_count": plant(jax.random.randint(streams_of[4], (COLS,), P_SIZE // 8, P_SIZE + 1), jax.random.fold_in(streams_of[4], 1), P_SIZE // 8, P_SIZE).astype(jnp.int32),
        "tile_counts": draw_tile_counts(jax.random.fold_in(streams_of[6], 71), 0),
    }


HIGHEST = lax.Precision.HIGHEST

def prepare(departures, innovations, precision, obs_count):
    row_ids = jnp.arange(departures.shape[1], dtype=jnp.int32)
    weight = jnp.where(row_ids[None, :] < obs_count[:, None], jnp.sqrt(precision), jnp.float32(0.0))
    scaled = (departures.astype(jnp.float32) * weight[:, :, None]).astype(jnp.bfloat16)
    signal = (weight * innovations).astype(jnp.bfloat16)
    return (scaled, signal)

def analyse(columns, scaled, signal):
    members = columns.shape[0]
    states = columns.astype(jnp.float32)
    average = lax.optimization_barrier(jnp.mean(states, axis=0))
    spread = (states - average[None]).astype(jnp.bfloat16)
    scaled_f = scaled.astype(jnp.float32)
    gram_matrix = jnp.einsum('npk,npj->nkj', scaled_f, scaled_f, precision=HIGHEST)
    pull_term = jnp.einsum('npk,np->nk', scaled_f, signal.astype(jnp.float32), precision=HIGHEST)
    identity = jnp.eye(members, dtype=jnp.float32)
    system = gram_matrix + (members - 1.0) * identity
    scale_norm = jnp.sqrt(lax.optimization_barrier(jnp.sum(system * system, axis=(1, 2))))
    root_iter = system / scale_norm[:, None, None]
    inverse_iter = jnp.broadcast_to(identity, system.shape)
    for repeat in range(ITERS):
        factor = 1.5 * identity - 0.5 * jnp.einsum('nij,njk->nik', inverse_iter, root_iter, precision=HIGHEST)
        if repeat + 1 < ITERS:
            root_iter = jnp.einsum('nij,njk->nik', root_iter, factor, precision=HIGHEST)
        inverse_iter = jnp.einsum('nij,njk->nik', factor, inverse_iter, precision=HIGHEST)
    halfway = jnp.einsum('njk,nk->nj', inverse_iter, pull_term, precision=HIGHEST)
    shift_w = jnp.einsum('njk,nk->nj', inverse_iter, halfway, precision=HIGHEST) / scale_norm[:, None]
    transform = (jnp.sqrt((members - 1.0) / scale_norm)[:, None, None] * inverse_iter + shift_w[:, :, None]).astype(jnp.bfloat16)
    update = jnp.einsum('njk,jnv->knv', transform.astype(jnp.float32), spread.astype(jnp.float32), precision=HIGHEST)
    return (average[None] + update).astype(jnp.bfloat16)

def reference(ensemble, departures, innovations, precision, obs_count, tile_counts):
    blocks = COLS // LOC
    states = ensemble.reshape(K, blocks, LOC, V).transpose(1, 0, 2, 3)

    def one_block(pieces):
        block_states, block_dep, block_inn, block_prec, block_count = pieces
        scaled, signal = prepare(block_dep, block_inn, block_prec, block_count)
        return analyse(block_states, scaled, signal)
    analysed = lax.map(one_block, (states, departures.reshape(blocks, LOC, P_SIZE, K), innovations.reshape(blocks, LOC, P_SIZE), precision.reshape(blocks, LOC, P_SIZE), obs_count.reshape(blocks, LOC)))
    analysed = analysed.transpose(1, 0, 2, 3).reshape(K, COLS, V)
    column_ids = jnp.arange(COLS, dtype=jnp.int32)
    tile_of = (column_ids // (N_MEMBER * LOC)).astype(jnp.int32)
    is_live = N_MEMBER * (column_ids % LOC) < jnp.take(tile_counts, tile_of)
    return jnp.where(is_live[None, :, None], analysed, ensemble)
```

```python
import jax
import jax.numpy as jnp
from jax import lax
from jax.sharding import PartitionSpec as P

WORK = 2
ITERS = 6


HIGHEST = lax.Precision.HIGH


def prepare(departures, innovations, precision, obs_count):
    row_ids = jnp.arange(departures.shape[1], dtype=jnp.int32)
    weight = jnp.where(row_ids[None, :] < obs_count[:, None], jnp.sqrt(precision), jnp.float32(0.0))
    scaled = (departures.astype(jnp.float32) * weight[:, :, None]).astype(jnp.bfloat16)
    signal = (weight * innovations).astype(jnp.bfloat16)
    return (scaled, signal)


def analyse(columns, scaled, signal):
    members = columns.shape[0]
    average = jnp.mean(columns.astype(jnp.float32), axis=0)
    spread = (columns.astype(jnp.float32) - average[None]).astype(jnp.bfloat16)
    gram_matrix = jnp.einsum("npk,npj->nkj", scaled, scaled, preferred_element_type=jnp.float32)
    pull_term = jnp.einsum("npk,np->nk", scaled, signal, preferred_element_type=jnp.float32)
    identity = jnp.eye(members, dtype=jnp.float32)
    system = gram_matrix + (members - 1.0) * identity
    scale_norm = jnp.sqrt(jnp.sum(system * system, axis=(1, 2)))
    root_iter = system / scale_norm[:, None, None]
    inverse_iter = jnp.broadcast_to(identity, system.shape)
    for repeat in range(ITERS):
        factor = 1.5 * identity - 0.5 * jnp.einsum(
            "nij,njk->nik", inverse_iter, root_iter, precision=HIGHEST
        )
        if repeat + 1 < ITERS:
            root_iter = jnp.einsum("nij,njk->nik", root_iter, factor, precision=HIGHEST)
        inverse_iter = jnp.einsum("nij,njk->nik", factor, inverse_iter, precision=HIGHEST)
    halfway = jnp.einsum("njk,nk->nj", inverse_iter, pull_term, precision=HIGHEST)
    shift_w = (
        jnp.einsum("njk,nk->nj", inverse_iter, halfway, precision=HIGHEST) / scale_norm[:, None]
    )
    transform = (
        jnp.sqrt((members - 1.0) / scale_norm)[:, None, None] * inverse_iter + shift_w[:, :, None]
    ).astype(jnp.bfloat16)
    update = jnp.einsum("njk,jnv->knv", transform, spread, preferred_element_type=jnp.float32)
    return (average[None] + update).astype(jnp.bfloat16)


def plan_indices(tile_counts, groups, capacity):
    margin = WORK // 2
    per_tile = tile_counts // groups
    tile_ids = jnp.arange(per_tile.shape[0], dtype=jnp.int32)
    before_sum = jnp.cumsum(per_tile) - per_tile
    tile_here = lax.axis_index("tile")
    lead_gap = jnp.take(before_sum - tile_ids * WORK, tile_here)
    trail_gap = jnp.take(before_sum + per_tile - (tile_ids + 1) * WORK, tile_here)
    count_here = jnp.take(per_tile, tile_here)
    positions = jnp.arange(capacity, dtype=jnp.int32)
    is_live = positions < count_here
    margin_ids = jnp.arange(margin, dtype=jnp.int32)
    send_index = jnp.clip(
        jnp.concatenate([margin_ids, WORK - lead_gap + margin_ids]), 0, capacity - 1
    )
    work_ids = jnp.arange(WORK, dtype=jnp.int32)
    take_index = jnp.where(
        work_ids < jnp.maximum(lead_gap, 0),
        capacity + work_ids,
        jnp.where(
            work_ids >= WORK + jnp.minimum(trail_gap, 0),
            capacity + margin + work_ids - WORK - trail_gap,
            work_ids - lead_gap,
        ),
    )
    take_index = jnp.clip(take_index, 0, capacity + 2 * margin - 1)
    return_index = jnp.clip(
        jnp.concatenate([margin_ids, WORK + trail_gap + margin_ids]), 0, WORK - 1
    )
    home_index = jnp.where(
        positions < jnp.maximum(-lead_gap, 0),
        WORK + positions,
        jnp.where(
            positions >= WORK - lead_gap, margin + positions + lead_gap, positions + lead_gap
        ),
    )
    home_index = jnp.clip(home_index, 0, WORK + 2 * margin - 1)
    return (is_live, send_index, take_index, return_index, home_index)


def pick(index, slots):
    picked = slots[-1]
    for slot in range(len(slots) - 2, -1, -1):
        picked = jnp.where(index == slot, slots[slot], picked)
    return picked


def shift_tiles(to_left, to_right):
    tiles = lax.axis_size("tile")
    from_right = lax.ppermute(to_left, "tile", [(t, t - 1) for t in range(1, tiles)])
    from_left = lax.ppermute(to_right, "tile", [(t, t + 1) for t in range(tiles - 1)])
    return from_left, from_right


def on_device(ensemble, departures, innovations, precision, obs_count, tile_counts):
    groups = lax.axis_size("member")
    part_rows = ensemble.shape[0]
    column_len = ensemble.shape[2]
    capacity = departures.shape[0]
    members = departures.shape[2]
    scaled, signal = prepare(departures, innovations, precision, obs_count)
    is_live, send_index, take_index, return_index, home_index = plan_indices(
        tile_counts, groups, capacity
    )

    def balance(slots):
        lefts, rights = shift_tiles(pick(send_index[0], slots), pick(send_index[1], slots))
        every = slots + [lefts, rights]
        return [pick(take_index[w], every) for w in range(WORK)]

    scaled2 = jnp.stack(balance([scaled[i] for i in range(capacity)]))
    signal2 = jnp.stack(balance([signal[i] for i in range(capacity)]))
    blocked = ensemble.reshape(part_rows, groups, capacity, column_len).transpose(2, 1, 0, 3)
    own = [blocked[i] for i in range(capacity)]
    work = balance(own)
    packed = jnp.stack(work, axis=1)
    columns = lax.all_to_all(packed, "member", split_axis=0, concat_axis=0, tiled=True)
    columns = columns.transpose(0, 2, 1, 3).reshape(members, WORK, column_len)
    result = analyse(columns, scaled2, signal2)
    result = result.reshape(groups, part_rows, WORK, column_len).transpose(0, 2, 1, 3)
    back = lax.all_to_all(result, "member", split_axis=0, concat_axis=0, tiled=True)
    home = [back[:, w] for w in range(WORK)]
    lefts, rights = shift_tiles(pick(return_index[0], home), pick(return_index[1], home))
    every = home + [lefts, rights]
    outs = [
        jnp.where(is_live[i], pick(home_index[i], every), own[i]) for i in range(capacity)
    ]
    out = jnp.stack(outs, axis=0).transpose(2, 1, 0, 3)
    return out.reshape(part_rows, groups * capacity, column_len)


def solution(mesh):
    placed = (
        P("member", "tile", None),
        P(("tile", "member"), None, None),
        P(("tile", "member"), None),
        P(("tile", "member"), None),
        P(("tile", "member")),
        P(),
    )
    return jax.shard_map(
        on_device, mesh=mesh, in_specs=placed, out_specs=P("member", "tile", None), check_vma=False
    )
```

```python
import functools

import jax
import jax.numpy as jnp
from jax import lax
from jax.experimental import pallas as pl
from jax.experimental.pallas import tpu as pltpu
from jax.sharding import PartitionSpec as P

WORK = 2
ITERS = 6
SLOTS = WORK + 2
PASSES = (1, 1, 1, 3, 3)
MESH = pl.DeviceIdType.MESH
F32 = jnp.float32
BF16 = jnp.bfloat16


def dot(a, b, ca=1, cb=0):
    return lax.dot_general(a, b, (((ca,), (cb,)), ((), ())), preferred_element_type=F32)


def split(x):
    high = x.astype(BF16)
    return high, (x - high.astype(F32)).astype(BF16)


def mm(a, b, passes):
    if passes == 1:
        return dot(a.astype(BF16), b.astype(BF16))
    ah, al = split(a)
    bh, bl = split(b)
    return dot(ah, bh) + (dot(ah, bl) + dot(al, bh))


def mm_exact(a, b):
    ah, al = split(a)
    return dot(ah, b) + dot(al, b)


def log2(n):
    return n.bit_length() - 1


def kernel(
    tiles, groups, counts_ref, obs_ref, ens_ref, dep_ref, inn_ref, prec_ref, out_ref,
    work, mrg_send, mrg_recv, obs_send, obs_recv, cols, ret, home,
    mrg_ssem, mrg_rsem, obs_ssem, obs_rsem, in_ssem, in_rsem, out_ssem, out_rsem, fwd_ssem, fwd_rsem,
):
    me = lax.axis_index("member")
    tile = lax.axis_index("tile")
    rows, width, length = ens_ref.shape
    capacity, obs_rows, members = dep_ref.shape
    has_left = tile > 0
    has_right = tile < tiles - 1

    barrier = pltpu.get_barrier_semaphore()
    for step in range(1, groups):
        peer = lax.rem(me + step, groups)
        pl.semaphore_signal(barrier, inc=1, device_id=(peer, tile), device_id_type=MESH)

    @pl.when(has_left)
    def _():
        pl.semaphore_signal(barrier, inc=1, device_id=(me, tile - 1), device_id_type=MESH)

    @pl.when(has_right)
    def _():
        pl.semaphore_signal(barrier, inc=1, device_id=(me, tile + 1), device_id_type=MESH)

    before = 0
    here = 0
    for other in range(tiles):
        count = counts_ref[other]
        before = before + jnp.where(other < tile, count, 0)
        here = here + jnp.where(other == tile, count, 0)
    before = before // groups
    here = here // groups
    lead = before - tile * WORK
    trail = before + here - (tile + 1) * WORK
    top = capacity - 1
    own = [jnp.clip(w - lead, 0, top) for w in range(WORK)]
    send_right = jnp.clip(WORK - lead, 0, top)
    from_left = lead > 0
    from_right = trail < 0

    eye_obs = lax.broadcasted_iota(jnp.int32, (obs_rows, obs_rows), 0) == lax.broadcasted_iota(
        jnp.int32, (obs_rows, obs_rows), 1
    )
    row_ids = lax.broadcasted_iota(jnp.int32, (1, obs_rows), 1)

    def observe(index):
        weight = jnp.where(row_ids < obs_ref[index], jnp.sqrt(prec_ref[pl.ds(index, 1), :]), 0.0)
        signal = weight * inn_ref[pl.ds(index, 1), :]
        weight_col = jnp.sum(jnp.where(eye_obs, weight, 0.0), axis=1, keepdims=True)
        scaled = dep_ref[index].astype(F32) * weight_col
        return scaled, jnp.broadcast_to(signal, (16, obs_rows))

    for side, index in enumerate((0, send_right)):
        scaled, signal = observe(index)
        obs_send[side, :obs_rows, :] = scaled.astype(BF16)
        obs_send[side, obs_rows:, :] = jnp.zeros((16, members), BF16)
        obs_send[side, obs_rows:, :obs_rows] = signal.astype(BF16)

    chunk = min(16, rows)
    lc, lg, lw, lcap = log2(chunk), log2(groups), log2(width), log2(capacity)
    block = groups * chunk
    out_row = lax.broadcasted_iota(jnp.int32, (SLOTS * block, 1), 0)
    slot = out_row >> (lc + lg)
    column = jnp.where(
        slot == 0, own[0], jnp.where(slot == 1, own[1], jnp.where(slot == 2, 0, send_right))
    )
    wanted = (
        ((out_row & (chunk - 1)) << lw) + (((out_row >> lc) & (groups - 1)) << lcap) + column
    )
    in_row = lax.broadcasted_iota(jnp.int32, (SLOTS * block, chunk * width), 1)
    gather = jnp.where(in_row == wanted, 1.0, 0.0).astype(BF16)
    for part in range(rows // chunk):
        span = pl.ds(part * chunk, chunk)
        states = ens_ref[span].reshape(chunk * width, length)
        picked = dot(gather, states)
        for s in range(SLOTS):
            piece = picked[s * block:(s + 1) * block].reshape(groups, chunk, length).astype(BF16)
            if s < WORK:
                work[:, s, span, :] = piece
            else:
                mrg_send[s - WORK, :, span, :] = piece

    @pl.when(jnp.logical_not(has_left))
    def _():
        mrg_recv[0] = jnp.zeros(mrg_recv.shape[1:], BF16)
        obs_recv[0] = jnp.zeros(obs_recv.shape[1:], BF16)
        home[WORK] = jnp.zeros(home.shape[1:], BF16)

    @pl.when(jnp.logical_not(has_right))
    def _():
        mrg_recv[1] = jnp.zeros(mrg_recv.shape[1:], BF16)
        obs_recv[1] = jnp.zeros(obs_recv.shape[1:], BF16)
        home[WORK + 1] = jnp.zeros(home.shape[1:], BF16)

    pl.semaphore_wait(
        barrier, groups - 1 + jnp.where(has_left, 1, 0) + jnp.where(has_right, 1, 0)
    )

    def remote(src, dst, ssem, rsem, device):
        return pltpu.make_async_remote_copy(
            src_ref=src, dst_ref=dst, send_sem=ssem, recv_sem=rsem,
            device_id=device, device_id_type=MESH,
        )

    def towards(side):
        return (me, tile - 1) if side == 0 else (me, tile + 1)

    sides = ((0, has_left, has_right), (1, has_right, has_left))

    def obs_copy(side):
        return remote(
            obs_send.at[side], obs_recv.at[1 - side], obs_ssem.at[side], obs_rsem.at[1 - side],
            towards(side),
        )

    def mrg_copy(side):
        return remote(
            mrg_send.at[side], mrg_recv.at[1 - side], mrg_ssem.at[side], mrg_rsem.at[1 - side],
            towards(side),
        )

    for side, sends, _ in sides:

        @pl.when(sends)
        def _(side=side):
            obs_copy(side).start()
            mrg_copy(side).start()

    ours = [observe(own[w]) for w in range(WORK)]

    for side, _, receives in sides:

        @pl.when(receives)
        def _(side=side):
            obs_copy(side).wait_recv()

    takes = (from_left, from_right)
    scaled, signal = [], []
    for w in range(WORK):
        took = jnp.where(takes[w], obs_recv[w, :obs_rows, :].astype(F32), ours[w][0])
        scaled.append(took.astype(BF16))
        took = jnp.where(takes[w], obs_recv[w, obs_rows:, :obs_rows].astype(F32), ours[w][1])
        signal.append(took.astype(BF16))

    for side, _, receives in sides:

        @pl.when(receives)
        def _(side=side):
            mrg_copy(side).wait_recv()

    for w in range(WORK):
        for g in range(groups):
            work[g, w] = jnp.where(
                takes[w], mrg_recv[w, g].astype(F32), work[g, w].astype(F32)
            ).astype(BF16)

    def in_copy(peer, source):
        return remote(
            work.at[peer], cols.at[source], in_ssem.at[peer], in_rsem.at[source], (peer, tile)
        )

    for step in range(1, groups):
        in_copy(lax.rem(me + step, groups), me).start()
    cols[me] = work[me]

    base = members - 1.0
    eye = jnp.where(eye_obs, 1.0, 0.0)
    both = range(WORK)
    gram = [dot(scaled[w], scaled[w], 1, 1) for w in both]
    norm, x, xc, pc, q, p = [], [], [], [], [], []
    for w in both:
        total = jnp.sum(
            gram[w] * gram[w] + (2.0 * base) * jnp.where(eye_obs, gram[w], 0.0), keepdims=True
        )
        norm.append(jnp.sqrt(total + base * base * members))
        x.append(gram[w] / norm[w])
        xc.append(base / norm[w])
        pc.append(1.5 - 0.5 * xc[w])
        q.append(-0.5 * eye)
        p.append(pc[w] * eye - 0.5 * x[w])
    for repeat in range(ITERS - 1):
        n_pass = PASSES[repeat]
        square = [mm(p[w], p[w], n_pass) for w in both]
        mixed = [
            mm(
                jnp.concatenate(
                    [square[w], square[w] + pc[w] * p[w] + (pc[w] * pc[w]) * eye], axis=1
                ),
                jnp.concatenate([p[w], xc[w] * q[w]], axis=0),
                n_pass,
            )
            for w in both
        ]
        for w in both:
            q[w] = 1.5 * q[w] - 0.5 * mixed[w]
            pc[w] = pc[w] * (1.5 - 0.5 * xc[w] * pc[w] * pc[w])
        if repeat + 2 < ITERS:
            p = [pc[w] * eye + mm(x[w], q[w], n_pass) for w in both]

    shift = []
    y = [signal[w].astype(F32) for w in both]
    for _ in range(2):
        y = [pc[w] * y[w] + mm(mm(y[w], q[w], 3), x[w], 3) for w in both]
    for w in both:
        shift.append(mm_exact(y[w], scaled[w])[:1] / norm[w])
    eye_all = lax.broadcasted_iota(jnp.int32, (members, members), 0) == lax.broadcasted_iota(
        jnp.int32, (members, members), 1
    )
    transform = []
    for w in both:
        half = mm_exact(q[w] / norm[w], scaled[w])
        hh, hl = split(half)
        inverse = dot(scaled[w], hh, 0, 0) + dot(scaled[w], hl, 0, 0)
        inverse = inverse + jnp.where(eye_all, pc[w], 0.0)
        transform.append((jnp.sqrt(base / norm[w]) * inverse + shift[w]).astype(BF16))

    for step in range(1, groups):
        in_copy(me, lax.rem(me + step, groups)).wait_recv()

    def out_copy(w, peer, source):
        return remote(
            ret.at[w, peer], home.at[w, source], out_ssem.at[w, peer], out_rsem.at[w, source],
            (peer, tile),
        )

    def fwd_copy(w, source):
        return remote(
            home.at[w, source], home.at[WORK + 1 - w, source],
            fwd_ssem.at[w, source], fwd_rsem.at[1 - w, source], towards(w),
        )

    for w in both:
        states = cols[:, w].astype(F32).reshape(members, length)
        average = jnp.sum(states, axis=0, keepdims=True) * (1.0 / members)
        spread = (states - average).astype(BF16)
        result = average + dot(transform[w], spread)
        ret[w] = result.reshape(groups, rows, length).astype(BF16)
        for step in range(1, groups):
            out_copy(w, lax.rem(me + step, groups), me).start()
        home[w, me] = ret[w, me]

    for step in range(groups):
        source = lax.rem(me + step, groups)
        for w, sends, _ in sides:
            if step:
                out_copy(w, me, source).wait_recv()

            @pl.when(sends)
            def _(w=w, source=source):
                fwd_copy(w, source).start()

    back_row = lax.broadcasted_iota(jnp.int32, (chunk * width, 1), 0)
    position = back_row & (capacity - 1)
    where_to = jnp.where(
        position < jnp.maximum(-lead, 0),
        WORK,
        jnp.where(position >= WORK - lead, WORK + 1, position + lead),
    )
    live = position < here
    target = (
        (where_to << (lc + lg))
        + (((back_row >> lcap) & (groups - 1)) << lc)
        + (back_row >> lw)
    )
    target = jnp.where(live, target, -1)
    home_row = lax.broadcasted_iota(jnp.int32, (chunk * width, SLOTS * block), 1)
    scatter = jnp.where(home_row == target, 1.0, 0.0).astype(BF16)

    for source in range(groups):
        for w, _, receives in sides:

            @pl.when(receives)
            def _(w=w, source=source):
                fwd_copy(w, source).wait_recv()

    for part in range(rows // chunk):
        span = pl.ds(part * chunk, chunk)
        parts = home[:, :, span, :].astype(F32).reshape(SLOTS * block, length).astype(BF16)
        placed = dot(scatter, parts)
        kept = ens_ref[span].reshape(chunk * width, length).astype(F32)
        placed = jnp.where(live, placed, kept)
        out_ref[span] = placed.astype(BF16).reshape(chunk, width, length)

    for side, sends, _ in sides:

        @pl.when(sends)
        def _(side=side):
            obs_copy(side).wait_send()
            mrg_copy(side).wait_send()
            for source in range(groups):
                fwd_copy(side, source).wait_send()

    for step in range(1, groups):
        peer = lax.rem(me + step, groups)
        in_copy(peer, me).wait_send()
        for w in both:
            out_copy(w, peer, me).wait_send()


def on_device(ensemble, departures, innovations, precision, obs_count, tile_counts):
    groups = lax.axis_size("member")
    tiles = lax.axis_size("tile")
    rows, width, length = ensemble.shape
    capacity, obs_rows, members = departures.shape
    vmem = pl.BlockSpec(memory_space=pltpu.VMEM)
    smem = pl.BlockSpec(memory_space=pltpu.SMEM)
    dma = pltpu.SemaphoreType.DMA
    return pl.pallas_call(
        functools.partial(kernel, tiles, groups),
        out_shape=jax.ShapeDtypeStruct(ensemble.shape, BF16),
        in_specs=[smem, smem, vmem, vmem, vmem, vmem],
        out_specs=vmem,
        scratch_shapes=[
            pltpu.VMEM((groups, WORK, rows, length), BF16),
            pltpu.VMEM((2, groups, rows, length), BF16),
            pltpu.VMEM((2, groups, rows, length), BF16),
            pltpu.VMEM((2, obs_rows + 16, members), BF16),
            pltpu.VMEM((2, obs_rows + 16, members), BF16),
            pltpu.VMEM((groups, WORK, rows, length), BF16),
            pltpu.VMEM((WORK, groups, rows, length), BF16),
            pltpu.VMEM((SLOTS, groups, rows, length), BF16),
            dma((2,)), dma((2,)), dma((2,)), dma((2,)),
            dma((groups,)), dma((groups,)),
            dma((WORK, groups)), dma((WORK, groups)),
            dma((WORK, groups)), dma((WORK, groups)),
        ],
        compiler_params=pltpu.CompilerParams(
            collective_id=0, has_side_effects=True, vmem_limit_bytes=56 * 1024 * 1024
        ),
    )(tile_counts, obs_count, ensemble, departures, innovations, precision)


def solution(mesh):
    placed = (
        P("member", "tile", None),
        P(("tile", "member"), None, None),
        P(("tile", "member"), None),
        P(("tile", "member"), None),
        P(("tile", "member")),
        P(),
    )
    return jax.shard_map(
        on_device, mesh=mesh, in_specs=placed, out_specs=P("member", "tile", None), check_vma=False
    )
```

```python
import functools

import jax
import jax.numpy as jnp
from jax import lax
from jax.experimental import pallas as pl
from jax.experimental.pallas import tpu as pltpu
from jax.sharding import PartitionSpec as P

WORK = 2
ITERS = 6
SLOTS = WORK + 2
PASSES = (1, 1, 1, 3, 3)
MESH = pl.DeviceIdType.MESH
F32 = jnp.float32
BF16 = jnp.bfloat16


def dot(a, b, ca=1, cb=0):
    return lax.dot_general(a, b, (((ca,), (cb,)), ((), ())), preferred_element_type=F32)


def split(x):
    high = x.astype(BF16)
    return high, (x - high.astype(F32)).astype(BF16)


def mm(a, b, passes):
    if passes == 1:
        return dot(a.astype(BF16), b.astype(BF16))
    ah, al = split(a)
    bh, bl = split(b)
    return dot(ah, bh) + (dot(ah, bl) + dot(al, bh))


def mm_exact(a, b):
    ah, al = split(a)
    return dot(ah, b) + dot(al, b)


def log2(n):
    return n.bit_length() - 1


def kernel(
    tiles, groups, counts_ref, obs_ref, ens_hbm, dep_hbm, inn_hbm, prec_hbm, out_ref,
    ens_ref, dep_ref, inn_ref, prec_ref, load_sem,
    work, mrg_send, mrg_recv, obs_send, obs_recv, cols, ret, home,
    mrg_ssem, mrg_rsem, obs_ssem, obs_rsem, in_ssem, in_rsem, out_ssem, out_rsem, fwd_ssem, fwd_rsem,
):
    me = lax.axis_index("member")
    tile = lax.axis_index("tile")
    loads = [
        pltpu.make_async_copy(source, kept, load_sem.at[i])
        for i, (source, kept) in enumerate(
            ((inn_hbm, inn_ref), (prec_hbm, prec_ref), (dep_hbm, dep_ref), (ens_hbm, ens_ref))
        )
    ]
    for load in loads:
        load.start()
    rows, width, length = ens_ref.shape
    capacity, obs_rows, members = dep_ref.shape
    has_left = tile > 0
    has_right = tile < tiles - 1

    barrier = pltpu.get_barrier_semaphore()
    for step in range(1, groups):
        peer = lax.rem(me + step, groups)
        pl.semaphore_signal(barrier, inc=1, device_id=(peer, tile), device_id_type=MESH)

    @pl.when(has_left)
    def _():
        pl.semaphore_signal(barrier, inc=1, device_id=(me, tile - 1), device_id_type=MESH)

    @pl.when(has_right)
    def _():
        pl.semaphore_signal(barrier, inc=1, device_id=(me, tile + 1), device_id_type=MESH)

    before = 0
    here = 0
    for other in range(tiles):
        count = counts_ref[other]
        before = before + jnp.where(other < tile, count, 0)
        here = here + jnp.where(other == tile, count, 0)
    before = before // groups
    here = here // groups
    lead = before - tile * WORK
    trail = before + here - (tile + 1) * WORK
    top = capacity - 1
    own = [jnp.clip(w - lead, 0, top) for w in range(WORK)]
    send_right = jnp.clip(WORK - lead, 0, top)
    from_left = lead > 0
    from_right = trail < 0

    eye_obs = lax.broadcasted_iota(jnp.int32, (obs_rows, obs_rows), 0) == lax.broadcasted_iota(
        jnp.int32, (obs_rows, obs_rows), 1
    )
    row_ids = lax.broadcasted_iota(jnp.int32, (1, obs_rows), 1)

    def observe(index):
        weight = jnp.where(row_ids < obs_ref[index], jnp.sqrt(prec_ref[pl.ds(index, 1), :]), 0.0)
        signal = weight * inn_ref[pl.ds(index, 1), :]
        weight_col = jnp.sum(jnp.where(eye_obs, weight, 0.0), axis=1, keepdims=True)
        scaled = dep_ref[index].astype(F32) * weight_col
        return scaled, jnp.broadcast_to(signal, (16, obs_rows))

    for load in loads[:3]:
        load.wait()
    for side, index in enumerate((0, send_right)):
        scaled, signal = observe(index)
        obs_send[side, :obs_rows, :] = scaled.astype(BF16)
        obs_send[side, obs_rows:, :] = jnp.zeros((16, members), BF16)
        obs_send[side, obs_rows:, :obs_rows] = signal.astype(BF16)

    chunk = min(16, rows)
    lc, lg, lw, lcap = log2(chunk), log2(groups), log2(width), log2(capacity)
    block = groups * chunk
    out_row = lax.broadcasted_iota(jnp.int32, (SLOTS * block, 1), 0)
    slot = out_row >> (lc + lg)
    column = jnp.where(
        slot == 0, own[0], jnp.where(slot == 1, own[1], jnp.where(slot == 2, 0, send_right))
    )
    wanted = (
        ((out_row & (chunk - 1)) << lw) + (((out_row >> lc) & (groups - 1)) << lcap) + column
    )
    in_row = lax.broadcasted_iota(jnp.int32, (SLOTS * block, chunk * width), 1)
    gather = jnp.where(in_row == wanted, 1.0, 0.0).astype(BF16)
    loads[3].wait()
    for part in range(rows // chunk):
        span = pl.ds(part * chunk, chunk)
        states = ens_ref[span].reshape(chunk * width, length)
        picked = dot(gather, states)
        for s in range(SLOTS):
            piece = picked[s * block:(s + 1) * block].reshape(groups, chunk, length).astype(BF16)
            if s < WORK:
                work[:, s, span, :] = piece
            else:
                mrg_send[s - WORK, :, span, :] = piece

    @pl.when(jnp.logical_not(has_left))
    def _():
        mrg_recv[0] = jnp.zeros(mrg_recv.shape[1:], BF16)
        obs_recv[0] = jnp.zeros(obs_recv.shape[1:], BF16)
        home[WORK] = jnp.zeros(home.shape[1:], BF16)

    @pl.when(jnp.logical_not(has_right))
    def _():
        mrg_recv[1] = jnp.zeros(mrg_recv.shape[1:], BF16)
        obs_recv[1] = jnp.zeros(obs_recv.shape[1:], BF16)
        home[WORK + 1] = jnp.zeros(home.shape[1:], BF16)

    pl.semaphore_wait(
        barrier, groups - 1 + jnp.where(has_left, 1, 0) + jnp.where(has_right, 1, 0)
    )

    def remote(src, dst, ssem, rsem, device):
        return pltpu.make_async_remote_copy(
            src_ref=src, dst_ref=dst, send_sem=ssem, recv_sem=rsem,
            device_id=device, device_id_type=MESH,
        )

    def towards(side):
        return (me, tile - 1) if side == 0 else (me, tile + 1)

    sides = ((0, has_left, has_right), (1, has_right, has_left))

    def obs_copy(side):
        return remote(
            obs_send.at[side], obs_recv.at[1 - side], obs_ssem.at[side], obs_rsem.at[1 - side],
            towards(side),
        )

    def mrg_copy(side):
        return remote(
            mrg_send.at[side], mrg_recv.at[1 - side], mrg_ssem.at[side], mrg_rsem.at[1 - side],
            towards(side),
        )

    for side, sends, _ in sides:

        @pl.when(sends)
        def _(side=side):
            obs_copy(side).start()
            mrg_copy(side).start()

    ours = [observe(own[w]) for w in range(WORK)]

    for side, _, receives in sides:

        @pl.when(receives)
        def _(side=side):
            obs_copy(side).wait_recv()

    takes = (from_left, from_right)
    scaled, signal = [], []
    for w in range(WORK):
        took = jnp.where(takes[w], obs_recv[w, :obs_rows, :].astype(F32), ours[w][0])
        scaled.append(took.astype(BF16))
        took = jnp.where(takes[w], obs_recv[w, obs_rows:, :obs_rows].astype(F32), ours[w][1])
        signal.append(took.astype(BF16))

    for side, _, receives in sides:

        @pl.when(receives)
        def _(side=side):
            mrg_copy(side).wait_recv()

    for w in range(WORK):
        for g in range(groups):
            work[g, w] = jnp.where(
                takes[w], mrg_recv[w, g].astype(F32), work[g, w].astype(F32)
            ).astype(BF16)

    def in_copy(peer, source):
        return remote(
            work.at[peer], cols.at[source], in_ssem.at[peer], in_rsem.at[source], (peer, tile)
        )

    @pl.when(me >= 0)
    def _():
        for step in range(1, groups):
            in_copy(lax.rem(me + step, groups), me).start()
        cols[me] = work[me]


    base = members - 1.0
    eye = jnp.where(eye_obs, 1.0, 0.0)
    both = range(WORK)
    gram = [dot(scaled[w], scaled[w], 1, 1) for w in both]
    norm, x, xc, pc, q, p = [], [], [], [], [], []
    for w in both:
        total = jnp.sum(
            gram[w] * gram[w] + (2.0 * base) * jnp.where(eye_obs, gram[w], 0.0), keepdims=True
        )
        norm.append(jnp.sqrt(total + base * base * members))
        x.append(gram[w] / norm[w])
        xc.append(base / norm[w])
        pc.append(1.5 - 0.5 * xc[w])
        q.append(-0.5 * eye)
        p.append(pc[w] * eye - 0.5 * x[w])
    for repeat in range(ITERS - 1):
        n_pass = PASSES[repeat]
        square = [mm(p[w], p[w], n_pass) for w in both]
        mixed = [
            mm(
                jnp.concatenate(
                    [square[w], square[w] + pc[w] * p[w] + (pc[w] * pc[w]) * eye], axis=1
                ),
                jnp.concatenate([p[w], xc[w] * q[w]], axis=0),
                n_pass,
            )
            for w in both
        ]
        for w in both:
            q[w] = 1.5 * q[w] - 0.5 * mixed[w]
            pc[w] = pc[w] * (1.5 - 0.5 * xc[w] * pc[w] * pc[w])
        if repeat + 2 < ITERS:
            p = [pc[w] * eye + mm(x[w], q[w], n_pass) for w in both]

    shift = []
    y = [signal[w].astype(F32) for w in both]
    for _ in range(2):
        y = [pc[w] * y[w] + mm(mm(y[w], q[w], 3), x[w], 3) for w in both]
    for w in both:
        shift.append(mm_exact(y[w], scaled[w])[:1] / norm[w])
    eye_all = lax.broadcasted_iota(jnp.int32, (members, members), 0) == lax.broadcasted_iota(
        jnp.int32, (members, members), 1
    )
    transform = []
    for w in both:
        half = mm_exact(q[w] / norm[w], scaled[w])
        hh, hl = split(half)
        inverse = dot(scaled[w], hh, 0, 0) + dot(scaled[w], hl, 0, 0)
        inverse = inverse + jnp.where(eye_all, pc[w], 0.0)
        transform.append((jnp.sqrt(base / norm[w]) * inverse + shift[w]).astype(BF16))

    for step in range(1, groups):
        in_copy(me, lax.rem(me + step, groups)).wait_recv()

    def out_copy(w, peer, source):
        return remote(
            ret.at[w, peer], home.at[w, source], out_ssem.at[w, peer], out_rsem.at[w, source],
            (peer, tile),
        )

    def fwd_copy(w, source):
        return remote(
            home.at[w, source], home.at[WORK + 1 - w, source],
            fwd_ssem.at[w, source], fwd_rsem.at[1 - w, source], towards(w),
        )

    for w in both:
        states = cols[:, w].astype(F32).reshape(members, length)
        average = jnp.sum(states, axis=0, keepdims=True) * (1.0 / members)
        spread = (states - average).astype(BF16)
        result = average + dot(transform[w], spread)
        ret[w] = result.reshape(groups, rows, length).astype(BF16)
        for step in range(1, groups):
            out_copy(w, lax.rem(me + step, groups), me).start()
        home[w, me] = ret[w, me]

    for step in range(groups):
        source = lax.rem(me + step, groups)
        for w, sends, _ in sides:
            if step:
                out_copy(w, me, source).wait_recv()

            @pl.when(sends)
            def _(w=w, source=source):
                fwd_copy(w, source).start()

    back_row = lax.broadcasted_iota(jnp.int32, (chunk * width, 1), 0)
    position = back_row & (capacity - 1)
    where_to = jnp.where(
        position < jnp.maximum(-lead, 0),
        WORK,
        jnp.where(position >= WORK - lead, WORK + 1, position + lead),
    )
    live = position < here
    target = (
        (where_to << (lc + lg))
        + (((back_row >> lcap) & (groups - 1)) << lc)
        + (back_row >> lw)
    )
    target = jnp.where(live, target, -1)
    home_row = lax.broadcasted_iota(jnp.int32, (chunk * width, SLOTS * block), 1)
    scatter = jnp.where(home_row == target, 1.0, 0.0).astype(BF16)

    for source in range(groups):
        for w, _, receives in sides:

            @pl.when(receives)
            def _(w=w, source=source):
                fwd_copy(w, source).wait_recv()

    for part in range(rows // chunk):
        span = pl.ds(part * chunk, chunk)
        parts = home[:, :, span, :].astype(F32).reshape(SLOTS * block, length).astype(BF16)
        placed = dot(scatter, parts)
        kept = ens_ref[span].reshape(chunk * width, length).astype(F32)
        placed = jnp.where(live, placed, kept)
        out_ref[span] = placed.astype(BF16).reshape(chunk, width, length)

    for side, sends, _ in sides:

        @pl.when(sends)
        def _(side=side):
            obs_copy(side).wait_send()
            mrg_copy(side).wait_send()
            for source in range(groups):
                fwd_copy(side, source).wait_send()

    for step in range(1, groups):
        peer = lax.rem(me + step, groups)
        in_copy(peer, me).wait_send()
        for w in both:
            out_copy(w, peer, me).wait_send()


def on_device(ensemble, departures, innovations, precision, obs_count, tile_counts):
    groups = lax.axis_size("member")
    tiles = lax.axis_size("tile")
    rows, width, length = ensemble.shape
    capacity, obs_rows, members = departures.shape
    vmem = pl.BlockSpec(memory_space=pltpu.VMEM)
    smem = pl.BlockSpec(memory_space=pltpu.SMEM)
    hbm = pl.BlockSpec(memory_space=pl.ANY)
    dma = pltpu.SemaphoreType.DMA
    return pl.pallas_call(
        functools.partial(kernel, tiles, groups),
        out_shape=jax.ShapeDtypeStruct(ensemble.shape, BF16),
        in_specs=[smem, smem, hbm, hbm, hbm, hbm],
        out_specs=vmem,
        scratch_shapes=[
            pltpu.VMEM(ensemble.shape, BF16),
            pltpu.VMEM(departures.shape, BF16),
            pltpu.VMEM(innovations.shape, F32),
            pltpu.VMEM(precision.shape, F32),
            dma((4,)),
            pltpu.VMEM((groups, WORK, rows, length), BF16),
            pltpu.VMEM((2, groups, rows, length), BF16),
            pltpu.VMEM((2, groups, rows, length), BF16),
            pltpu.VMEM((2, obs_rows + 16, members), BF16),
            pltpu.VMEM((2, obs_rows + 16, members), BF16),
            pltpu.VMEM((groups, WORK, rows, length), BF16),
            pltpu.VMEM((WORK, groups, rows, length), BF16),
            pltpu.VMEM((SLOTS, groups, rows, length), BF16),
            dma((2,)), dma((2,)), dma((2,)), dma((2,)),
            dma((groups,)), dma((groups,)),
            dma((WORK, groups)), dma((WORK, groups)),
            dma((WORK, groups)), dma((WORK, groups)),
        ],
        compiler_params=pltpu.CompilerParams(
            collective_id=0, has_side_effects=True, vmem_limit_bytes=56 * 1024 * 1024
        ),
    )(tile_counts, obs_count, ensemble, departures, innovations, precision)


def solution(mesh):
    placed = (
        P("member", "tile", None),
        P(("tile", "member"), None, None),
        P(("tile", "member"), None),
        P(("tile", "member"), None),
        P(("tile", "member")),
        P(),
    )
    return jax.shard_map(
        on_device, mesh=mesh, in_specs=placed, out_specs=P("member", "tile", None), check_vma=False
    )
```

```python
import functools

import jax
import jax.numpy as jnp
from jax import lax
from jax.experimental import pallas as pl
from jax.experimental.pallas import tpu as pltpu
from jax.sharding import PartitionSpec as P

WORK = 2
ITERS = 6
SLOTS = WORK + 2
PASSES = (1, 1, 1, 3, 3)
MESH = pl.DeviceIdType.MESH
F32 = jnp.float32
BF16 = jnp.bfloat16


def dot(a, b, ca=1, cb=0):
    return lax.dot_general(a, b, (((ca,), (cb,)), ((), ())), preferred_element_type=F32)


def split(x):
    high = x.astype(BF16)
    return high, (x - high.astype(F32)).astype(BF16)


def mm(a, b, passes):
    if passes == 1:
        return dot(a.astype(BF16), b.astype(BF16))
    ah, al = split(a)
    bh, bl = split(b)
    return dot(ah, bh) + (dot(ah, bl) + dot(al, bh))


def mm_exact(a, b):
    ah, al = split(a)
    return dot(ah, b) + dot(al, b)


def log2(n):
    return n.bit_length() - 1


def kernel(
    tiles, groups, counts_ref, obs_ref, ens_hbm, dep_hbm, inn_hbm, prec_hbm, out_ref,
    ens_ref, dep_ref, inn_ref, prec_ref, load_sem,
    work, mrg_send, mrg_recv, obs_send, obs_recv, cols, ret, home,
    mrg_ssem, mrg_rsem, obs_ssem, obs_rsem, in_ssem, in_rsem, out_ssem, out_rsem, fwd_ssem, fwd_rsem,
):
    me = lax.axis_index("member")
    tile = lax.axis_index("tile")
    loads = [
        pltpu.make_async_copy(source, kept, load_sem.at[i])
        for i, (source, kept) in enumerate(
            ((inn_hbm, inn_ref), (prec_hbm, prec_ref), (dep_hbm, dep_ref), (ens_hbm, ens_ref))
        )
    ]
    for load in loads:
        load.start()
    rows, width, length = ens_ref.shape
    capacity, obs_rows, members = dep_ref.shape
    has_left = tile > 0
    has_right = tile < tiles - 1

    barrier = pltpu.get_barrier_semaphore()
    for step in range(1, groups):
        peer = lax.rem(me + step, groups)
        pl.semaphore_signal(barrier, inc=1, device_id=(peer, tile), device_id_type=MESH)

    @pl.when(has_left)
    def _():
        pl.semaphore_signal(barrier, inc=1, device_id=(me, tile - 1), device_id_type=MESH)

    @pl.when(has_right)
    def _():
        pl.semaphore_signal(barrier, inc=1, device_id=(me, tile + 1), device_id_type=MESH)

    before = 0
    here = 0
    for other in range(tiles):
        count = counts_ref[other]
        before = before + jnp.where(other < tile, count, 0)
        here = here + jnp.where(other == tile, count, 0)
    before = before // groups
    here = here // groups
    lead = before - tile * WORK
    trail = before + here - (tile + 1) * WORK
    top = capacity - 1
    own = [jnp.clip(w - lead, 0, top) for w in range(WORK)]
    send_right = jnp.clip(WORK - lead, 0, top)
    from_left = lead > 0
    from_right = trail < 0

    eye_obs = lax.broadcasted_iota(jnp.int32, (obs_rows, obs_rows), 0) == lax.broadcasted_iota(
        jnp.int32, (obs_rows, obs_rows), 1
    )
    row_ids = lax.broadcasted_iota(jnp.int32, (1, obs_rows), 1)

    def observe(index):
        weight = jnp.where(row_ids < obs_ref[index], jnp.sqrt(prec_ref[pl.ds(index, 1), :]), 0.0)
        signal = weight * inn_ref[pl.ds(index, 1), :]
        weight_col = jnp.sum(jnp.where(eye_obs, weight, 0.0), axis=1, keepdims=True)
        scaled = dep_ref[index].astype(F32) * weight_col
        return scaled, jnp.broadcast_to(signal, (16, obs_rows))

    for load in loads[:3]:
        load.wait()
    for side, index in enumerate((0, send_right)):
        scaled, signal = observe(index)
        obs_send[side, :obs_rows, :] = scaled.astype(BF16)
        obs_send[side, obs_rows:, :] = jnp.zeros((16, members), BF16)
        obs_send[side, obs_rows:, :obs_rows] = signal.astype(BF16)

    chunk = min(16, rows)
    lc, lg, lw, lcap = log2(chunk), log2(groups), log2(width), log2(capacity)
    block = groups * chunk
    out_row = lax.broadcasted_iota(jnp.int32, (SLOTS * block, 1), 0)
    slot = out_row >> (lc + lg)
    column = jnp.where(
        slot == 0, own[0], jnp.where(slot == 1, own[1], jnp.where(slot == 2, 0, send_right))
    )
    wanted = (
        ((out_row & (chunk - 1)) << lw) + (((out_row >> lc) & (groups - 1)) << lcap) + column
    )
    in_row = lax.broadcasted_iota(jnp.int32, (SLOTS * block, chunk * width), 1)
    gather = jnp.where(in_row == wanted, 1.0, 0.0).astype(BF16)
    loads[3].wait()
    for part in range(rows // chunk):
        span = pl.ds(part * chunk, chunk)
        states = ens_ref[span].reshape(chunk * width, length)
        picked = dot(gather, states)
        for s in range(SLOTS):
            piece = picked[s * block:(s + 1) * block].reshape(groups, chunk, length).astype(BF16)
            if s < WORK:
                work[:, s, span, :] = piece
            else:
                mrg_send[s - WORK, :, span, :] = piece

    @pl.when(jnp.logical_not(has_left))
    def _():
        mrg_recv[0] = jnp.zeros(mrg_recv.shape[1:], BF16)
        obs_recv[0] = jnp.zeros(obs_recv.shape[1:], BF16)
        home[WORK] = jnp.zeros(home.shape[1:], BF16)

    @pl.when(jnp.logical_not(has_right))
    def _():
        mrg_recv[1] = jnp.zeros(mrg_recv.shape[1:], BF16)
        obs_recv[1] = jnp.zeros(obs_recv.shape[1:], BF16)
        home[WORK + 1] = jnp.zeros(home.shape[1:], BF16)

    pl.semaphore_wait(
        barrier, groups - 1 + jnp.where(has_left, 1, 0) + jnp.where(has_right, 1, 0)
    )

    def remote(src, dst, ssem, rsem, device):
        return pltpu.make_async_remote_copy(
            src_ref=src, dst_ref=dst, send_sem=ssem, recv_sem=rsem,
            device_id=device, device_id_type=MESH,
        )

    def towards(side):
        return (me, tile - 1) if side == 0 else (me, tile + 1)

    sides = ((0, has_left, has_right), (1, has_right, has_left))

    def obs_copy(side):
        return remote(
            obs_send.at[side], obs_recv.at[1 - side], obs_ssem.at[side], obs_rsem.at[1 - side],
            towards(side),
        )

    def mrg_copy(side):
        return remote(
            mrg_send.at[side], mrg_recv.at[1 - side], mrg_ssem.at[side], mrg_rsem.at[1 - side],
            towards(side),
        )

    for side, sends, _ in sides:

        @pl.when(sends)
        def _(side=side):
            obs_copy(side).start()
            mrg_copy(side).start()

    ours = [observe(own[w]) for w in range(WORK)]

    for side, _, receives in sides:

        @pl.when(receives)
        def _(side=side):
            obs_copy(side).wait_recv()

    takes = (from_left, from_right)
    scaled, signal = [], []
    for w in range(WORK):
        took = jnp.where(takes[w], obs_recv[w, :obs_rows, :].astype(F32), ours[w][0])
        scaled.append(took.astype(BF16))
        took = jnp.where(takes[w], obs_recv[w, obs_rows:, :obs_rows].astype(F32), ours[w][1])
        signal.append(took.astype(BF16))

    for side, _, receives in sides:

        @pl.when(receives)
        def _(side=side):
            mrg_copy(side).wait_recv()

    for w in range(WORK):
        for g in range(groups):
            work[g, w] = jnp.where(
                takes[w], mrg_recv[w, g].astype(F32), work[g, w].astype(F32)
            ).astype(BF16)

    def in_copy(peer, source):
        return remote(
            work.at[peer], cols.at[source], in_ssem.at[peer], in_rsem.at[source], (peer, tile)
        )

    @pl.when(me >= 0)
    def _():
        for step in range(1, groups):
            in_copy(lax.rem(me + step, groups), me).start()
        cols[me] = work[me]


    base = members - 1.0
    eye = jnp.where(eye_obs, 1.0, 0.0)
    both = range(WORK)
    gram = [dot(scaled[w], scaled[w], 1, 1) for w in both]
    norm, x, xc, pc, q, p = [], [], [], [], [], []
    for w in both:
        total = jnp.sum(
            gram[w] * gram[w] + (2.0 * base) * jnp.where(eye_obs, gram[w], 0.0), keepdims=True
        )
        norm.append(jnp.sqrt(total + base * base * members))
        x.append(gram[w] / norm[w])
        xc.append(base / norm[w])
        pc.append(1.5 - 0.5 * xc[w])
        q.append(-0.5 * eye)
        p.append(pc[w] * eye - 0.5 * x[w])
    for repeat in range(ITERS - 1):
        n_pass = PASSES[repeat]
        square = [mm(p[w], p[w], n_pass) for w in both]
        mixed = [
            mm(
                jnp.concatenate(
                    [square[w], square[w] + pc[w] * p[w] + (pc[w] * pc[w]) * eye], axis=1
                ),
                jnp.concatenate([p[w], xc[w] * q[w]], axis=0),
                n_pass,
            )
            for w in both
        ]
        for w in both:
            q[w] = 1.5 * q[w] - 0.5 * mixed[w]
            pc[w] = pc[w] * (1.5 - 0.5 * xc[w] * pc[w] * pc[w])
        if repeat + 2 < ITERS:
            p = [pc[w] * eye + mm(x[w], q[w], n_pass) for w in both]

    shift = []
    y = [signal[w].astype(F32) for w in both]
    for _ in range(2):
        y = [pc[w] * y[w] + mm(mm(y[w], q[w], 3), x[w], 3) for w in both]
    for w in both:
        shift.append(mm_exact(y[w], scaled[w])[:1] / norm[w])
    eye_all = lax.broadcasted_iota(jnp.int32, (members, members), 0) == lax.broadcasted_iota(
        jnp.int32, (members, members), 1
    )
    transform = []
    for w in both:
        half = mm_exact(q[w] / norm[w], scaled[w])
        hh, hl = split(half)
        inverse = dot(scaled[w], hh, 0, 0) + dot(scaled[w], hl, 0, 0)
        inverse = inverse + jnp.where(eye_all, pc[w], 0.0)
        transform.append((jnp.sqrt(base / norm[w]) * inverse + shift[w]).astype(BF16))

    for step in range(1, groups):
        in_copy(me, lax.rem(me + step, groups)).wait_recv()

    def out_copy(w, peer, source):
        return remote(
            ret.at[w, peer], home.at[w, source], out_ssem.at[w, peer], out_rsem.at[w, source],
            (peer, tile),
        )

    def fwd_copy(w, source):
        return remote(
            home.at[w, source], home.at[WORK + 1 - w, source],
            fwd_ssem.at[w, source], fwd_rsem.at[1 - w, source], towards(w),
        )

    for w in both:
        states = cols[:, w].astype(F32).reshape(members, length)
        average = jnp.sum(states, axis=0, keepdims=True) * (1.0 / members)
        spread = (states - average).astype(BF16)
        result = average + dot(transform[w], spread)
        ret[w] = result.reshape(groups, rows, length).astype(BF16)
        for step in range(1, groups):
            out_copy(w, lax.rem(me + step, groups), me).start()
        home[w, me] = ret[w, me]

    for step in range(groups):
        source = lax.rem(me + step, groups)
        for w, sends, _ in sides:
            if step:
                out_copy(w, me, source).wait_recv()

            @pl.when(sends)
            def _(w=w, source=source):
                fwd_copy(w, source).start()

    back_row = lax.broadcasted_iota(jnp.int32, (chunk * width, 1), 0)
    position = back_row & (capacity - 1)
    where_to = jnp.where(
        position < jnp.maximum(-lead, 0),
        WORK,
        jnp.where(position >= WORK - lead, WORK + 1, position + lead),
    )
    live = position < here
    target = (
        (where_to << (lc + lg))
        + (((back_row >> lcap) & (groups - 1)) << lc)
        + (back_row >> lw)
    )
    target = jnp.where(live, target, -1)
    home_row = lax.broadcasted_iota(jnp.int32, (chunk * width, SLOTS * block), 1)
    scatter = jnp.where(home_row == target, 1.0, 0.0).astype(BF16)

    for source in range(groups):
        for w, _, receives in sides:

            @pl.when(receives)
            def _(w=w, source=source):
                fwd_copy(w, source).wait_recv()

    for part in range(rows // chunk):
        span = pl.ds(part * chunk, chunk)
        parts = home[:, :, span, :].astype(F32).reshape(SLOTS * block, length).astype(BF16)
        placed = dot(scatter, parts)
        kept = ens_ref[span].reshape(chunk * width, length).astype(F32)
        placed = jnp.where(live, placed, kept)
        out_ref[span] = placed.astype(BF16).reshape(chunk, width, length)

    for side, sends, _ in sides:

        @pl.when(sends)
        def _(side=side):
            obs_copy(side).wait_send()
            mrg_copy(side).wait_send()
            for source in range(groups):
                fwd_copy(side, source).wait_send()

    for step in range(1, groups):
        peer = lax.rem(me + step, groups)
        in_copy(peer, me).wait_send()
        for w in both:
            out_copy(w, peer, me).wait_send()


def on_device(ensemble, departures, innovations, precision, obs_count, tile_counts):
    groups = lax.axis_size("member")
    tiles = lax.axis_size("tile")
    rows, width, length = ensemble.shape
    capacity, obs_rows, members = departures.shape
    vmem = pl.BlockSpec(memory_space=pltpu.VMEM)
    smem = pl.BlockSpec(memory_space=pltpu.SMEM)
    hbm = pl.BlockSpec(memory_space=pl.ANY)
    dma = pltpu.SemaphoreType.DMA
    return pl.pallas_call(
        functools.partial(kernel, tiles, groups),
        out_shape=pltpu.VMEM(ensemble.shape, BF16),
        in_specs=[smem, smem, hbm, hbm, hbm, hbm],
        out_specs=vmem,
        scratch_shapes=[
            pltpu.VMEM(ensemble.shape, BF16),
            pltpu.VMEM(departures.shape, BF16),
            pltpu.VMEM(innovations.shape, F32),
            pltpu.VMEM(precision.shape, F32),
            dma((4,)),
            pltpu.VMEM((groups, WORK, rows, length), BF16),
            pltpu.VMEM((2, groups, rows, length), BF16),
            pltpu.VMEM((2, groups, rows, length), BF16),
            pltpu.VMEM((2, obs_rows + 16, members), BF16),
            pltpu.VMEM((2, obs_rows + 16, members), BF16),
            pltpu.VMEM((groups, WORK, rows, length), BF16),
            pltpu.VMEM((WORK, groups, rows, length), BF16),
            pltpu.VMEM((SLOTS, groups, rows, length), BF16),
            dma((2,)), dma((2,)), dma((2,)), dma((2,)),
            dma((groups,)), dma((groups,)),
            dma((WORK, groups)), dma((WORK, groups)),
            dma((WORK, groups)), dma((WORK, groups)),
        ],
        compiler_params=pltpu.CompilerParams(
            collective_id=0, has_side_effects=True, vmem_limit_bytes=56 * 1024 * 1024
        ),
    )(tile_counts, obs_count, ensemble, departures, innovations, precision)


def solution(mesh):
    placed = (
        P("member", "tile", None),
        P(("tile", "member"), None, None),
        P(("tile", "member"), None),
        P(("tile", "member"), None),
        P(("tile", "member")),
        P(),
    )
    return jax.shard_map(
        on_device, mesh=mesh, in_specs=placed, out_specs=P("member", "tile", None), check_vma=False
    )
```

```python
import functools

import jax
import jax.numpy as jnp
from jax import lax
from jax.experimental import pallas as pl
from jax.experimental.pallas import tpu as pltpu
from jax.sharding import PartitionSpec as P

WORK = 2
ITERS = 6
SLOTS = WORK + 2
PASSES = (1, 1, 1, 3, 3)
MESH = pl.DeviceIdType.MESH
F32 = jnp.float32
BF16 = jnp.bfloat16


def dot(a, b, ca=1, cb=0):
    return lax.dot_general(a, b, (((ca,), (cb,)), ((), ())), preferred_element_type=F32)


def split(x):
    high = x.astype(BF16)
    return high, (x - high.astype(F32)).astype(BF16)


def mm(a, b, passes):
    if passes == 1:
        return dot(a.astype(BF16), b.astype(BF16))
    ah, al = split(a)
    bh, bl = split(b)
    return dot(ah, bh) + (dot(ah, bl) + dot(al, bh))


def mm_exact(a, b):
    ah, al = split(a)
    return dot(ah, b) + dot(al, b)


def log2(n):
    return n.bit_length() - 1


def kernel(
    tiles, groups, counts_ref, obs_ref, ens_hbm, dep_hbm, inn_hbm, prec_hbm, out_ref,
    ens_ref, dep_ref, inn_ref, prec_ref, load_sem,
    work, mrg_send, mrg_recv, obs_send, obs_recv, cols, ret, home, home_left, home_right,
    mrg_ssem, mrg_rsem, obs_ssem, obs_rsem, in_ssem, in_rsem, out_ssem, out_rsem, fwd_ssem, fwd_rsem,
):
    me = lax.axis_index("member")
    tile = lax.axis_index("tile")
    loads = [
        pltpu.make_async_copy(source, kept, load_sem.at[i])
        for i, (source, kept) in enumerate(
            ((inn_hbm, inn_ref), (prec_hbm, prec_ref), (dep_hbm, dep_ref), (ens_hbm, ens_ref))
        )
    ]
    for load in loads:
        load.start()
    rows, width, length = ens_ref.shape
    capacity, obs_rows, members = dep_ref.shape
    low = length // 128 * 128
    high = -(-length // 128) * 128
    lanes = [pl.ds(w * length, length) for w in range(WORK)]
    has_left = tile > 0
    has_right = tile < tiles - 1

    barrier = pltpu.get_barrier_semaphore()
    for step in range(1, groups):
        peer = lax.rem(me + step, groups)
        pl.semaphore_signal(barrier, inc=1, device_id=(peer, tile), device_id_type=MESH)

    @pl.when(has_left)
    def _():
        pl.semaphore_signal(barrier, inc=1, device_id=(me, tile - 1), device_id_type=MESH)

    @pl.when(has_right)
    def _():
        pl.semaphore_signal(barrier, inc=1, device_id=(me, tile + 1), device_id_type=MESH)

    before = 0
    here = 0
    for other in range(tiles):
        count = counts_ref[other]
        before = before + jnp.where(other < tile, count, 0)
        here = here + jnp.where(other == tile, count, 0)
    before = before // groups
    here = here // groups
    lead = before - tile * WORK
    trail = before + here - (tile + 1) * WORK
    top = capacity - 1
    own = [jnp.clip(w - lead, 0, top) for w in range(WORK)]
    send_right = jnp.clip(WORK - lead, 0, top)
    from_left = lead > 0
    from_right = trail < 0

    eye_obs = lax.broadcasted_iota(jnp.int32, (obs_rows, obs_rows), 0) == lax.broadcasted_iota(
        jnp.int32, (obs_rows, obs_rows), 1
    )
    row_ids = lax.broadcasted_iota(jnp.int32, (1, obs_rows), 1)

    def observe(index):
        weight = jnp.where(row_ids < obs_ref[index], jnp.sqrt(prec_ref[pl.ds(index, 1), :]), 0.0)
        signal = weight * inn_ref[pl.ds(index, 1), :]
        weight_col = jnp.sum(jnp.where(eye_obs, weight, 0.0), axis=1, keepdims=True)
        scaled = dep_ref[index].astype(F32) * weight_col
        return scaled, jnp.broadcast_to(signal, (16, obs_rows))

    for load in loads[:3]:
        load.wait()
    for side, index in enumerate((0, send_right)):
        scaled, signal = observe(index)
        obs_send[side, :obs_rows, :] = scaled.astype(BF16)
        obs_send[side, obs_rows:, :] = jnp.zeros((16, members), BF16)
        obs_send[side, obs_rows:, :obs_rows] = signal.astype(BF16)

    chunk = min(16, rows)
    lc, lg, lw, lcap = log2(chunk), log2(groups), log2(width), log2(capacity)
    block = groups * chunk
    out_row = lax.broadcasted_iota(jnp.int32, (SLOTS * block, 1), 0)
    slot = out_row >> (lc + lg)
    column = jnp.where(
        slot == 0, own[0], jnp.where(slot == 1, own[1], jnp.where(slot == 2, 0, send_right))
    )
    wanted = (
        ((out_row & (chunk - 1)) << lw) + (((out_row >> lc) & (groups - 1)) << lcap) + column
    )
    in_row = lax.broadcasted_iota(jnp.int32, (SLOTS * block, chunk * width), 1)
    gather = jnp.where(in_row == wanted, 1.0, 0.0).astype(BF16)
    loads[3].wait()
    for part in range(rows // chunk):
        span = pl.ds(part * chunk, chunk)
        states = ens_ref[span].reshape(chunk * width, length)
        picked = dot(gather, states)
        for s in range(SLOTS):
            piece = picked[s * block:(s + 1) * block].reshape(groups, chunk, length).astype(BF16)
            if s < WORK:
                work[:, span, lanes[s]] = piece
            else:
                mrg_send[s - WORK, :, span, :] = piece

    @pl.when(jnp.logical_not(has_left))
    def _():
        mrg_recv[0] = jnp.zeros(mrg_recv.shape[1:], BF16)
        obs_recv[0] = jnp.zeros(obs_recv.shape[1:], BF16)
        home_left[...] = jnp.zeros(home_left.shape, BF16)

    @pl.when(jnp.logical_not(has_right))
    def _():
        mrg_recv[1] = jnp.zeros(mrg_recv.shape[1:], BF16)
        obs_recv[1] = jnp.zeros(obs_recv.shape[1:], BF16)
        home_right[...] = jnp.zeros(home_right.shape, BF16)

    pl.semaphore_wait(
        barrier, groups - 1 + jnp.where(has_left, 1, 0) + jnp.where(has_right, 1, 0)
    )

    def remote(src, dst, ssem, rsem, device):
        return pltpu.make_async_remote_copy(
            src_ref=src, dst_ref=dst, send_sem=ssem, recv_sem=rsem,
            device_id=device, device_id_type=MESH,
        )

    def towards(side):
        return (me, tile - 1) if side == 0 else (me, tile + 1)

    sides = ((0, has_left, has_right), (1, has_right, has_left))

    def obs_copy(side):
        return remote(
            obs_send.at[side], obs_recv.at[1 - side], obs_ssem.at[side], obs_rsem.at[1 - side],
            towards(side),
        )

    def mrg_copy(side):
        return remote(
            mrg_send.at[side], mrg_recv.at[1 - side], mrg_ssem.at[side], mrg_rsem.at[1 - side],
            towards(side),
        )

    for side, sends, _ in sides:

        @pl.when(sends)
        def _(side=side):
            obs_copy(side).start()
            mrg_copy(side).start()

    ours = [observe(own[w]) for w in range(WORK)]

    for side, _, receives in sides:

        @pl.when(receives)
        def _(side=side):
            obs_copy(side).wait_recv()

    takes = (from_left, from_right)
    scaled, signal = [], []
    for w in range(WORK):
        took = jnp.where(takes[w], obs_recv[w, :obs_rows, :].astype(F32), ours[w][0])
        scaled.append(took.astype(BF16))
        took = jnp.where(takes[w], obs_recv[w, obs_rows:, :obs_rows].astype(F32), ours[w][1])
        signal.append(took.astype(BF16))

    for side, _, receives in sides:

        @pl.when(receives)
        def _(side=side):
            mrg_copy(side).wait_recv()

    for w in range(WORK):
        for g in range(groups):
            work[g, :, lanes[w]] = jnp.where(
                takes[w], mrg_recv[w, g].astype(F32), work[g, :, lanes[w]].astype(F32)
            ).astype(BF16)

    def in_copy(peer, source):
        return remote(
            work.at[peer], cols.at[source], in_ssem.at[peer], in_rsem.at[source], (peer, tile)
        )

    @pl.when(me >= 0)
    def _():
        for step in range(1, groups):
            in_copy(lax.rem(me + step, groups), me).start()
        cols[me] = work[me]


    base = members - 1.0
    eye = jnp.where(eye_obs, 1.0, 0.0)
    both = range(WORK)
    gram = [dot(scaled[w], scaled[w], 1, 1) for w in both]
    norm, x, xc, pc, q, p = [], [], [], [], [], []
    for w in both:
        total = jnp.sum(
            gram[w] * gram[w] + (2.0 * base) * jnp.where(eye_obs, gram[w], 0.0), keepdims=True
        )
        norm.append(jnp.sqrt(total + base * base * members))
        x.append(gram[w] / norm[w])
        xc.append(base / norm[w])
        pc.append(1.5 - 0.5 * xc[w])
        q.append(-0.5 * eye)
        p.append(pc[w] * eye - 0.5 * x[w])
    for repeat in range(ITERS - 1):
        n_pass = PASSES[repeat]
        square = [mm(p[w], p[w], n_pass) for w in both]
        mixed = [
            mm(
                jnp.concatenate(
                    [square[w], square[w] + pc[w] * p[w] + (pc[w] * pc[w]) * eye], axis=1
                ),
                jnp.concatenate([p[w], xc[w] * q[w]], axis=0),
                n_pass,
            )
            for w in both
        ]
        for w in both:
            q[w] = 1.5 * q[w] - 0.5 * mixed[w]
            pc[w] = pc[w] * (1.5 - 0.5 * xc[w] * pc[w] * pc[w])
        if repeat + 2 < ITERS:
            p = [pc[w] * eye + mm(x[w], q[w], n_pass) for w in both]

    shift = []
    y = [signal[w].astype(F32) for w in both]
    for _ in range(2):
        y = [pc[w] * y[w] + mm(mm(y[w], q[w], 3), x[w], 3) for w in both]
    for w in both:
        shift.append(mm_exact(y[w], scaled[w])[:1] / norm[w])
    eye_all = lax.broadcasted_iota(jnp.int32, (members, members), 0) == lax.broadcasted_iota(
        jnp.int32, (members, members), 1
    )
    transform = []
    for w in both:
        half = mm_exact(q[w] / norm[w], scaled[w])
        hh, hl = split(half)
        inverse = dot(scaled[w], hh, 0, 0) + dot(scaled[w], hl, 0, 0)
        inverse = inverse + jnp.where(eye_all, pc[w], 0.0)
        transform.append((jnp.sqrt(base / norm[w]) * inverse + shift[w]).astype(BF16))

    for step in range(1, groups):
        in_copy(me, lax.rem(me + step, groups)).wait_recv()

    def out_copy(peer, source):
        return remote(
            ret.at[peer], home.at[source], out_ssem.at[peer], out_rsem.at[source], (peer, tile)
        )

    def fwd_copy(w, source):
        span = pl.ds(0, high) if w == 0 else pl.ds(low, 2 * length - low)
        return remote(
            home.at[source, :, span], (home_right if w == 0 else home_left).at[source],
            fwd_ssem.at[w, source], fwd_rsem.at[1 - w, source], towards(w),
        )

    for w in both:
        states = cols[:, :, lanes[w]].astype(F32).reshape(members, length)
        average = jnp.sum(states, axis=0, keepdims=True) * (1.0 / members)
        spread = (states - average).astype(BF16)
        result = average + dot(transform[w], spread)
        ret[:, :, lanes[w]] = result.reshape(groups, rows, length).astype(BF16)

    @pl.when(me >= 0)
    def _():
        for step in range(1, groups):
            out_copy(lax.rem(me + step, groups), me).start()
        home[me] = ret[me]

    for step in range(groups):
        source = lax.rem(me + step, groups)
        if step:
            out_copy(me, source).wait_recv()
        for w, sends, _ in sides:

            @pl.when(sends)
            def _(w=w, source=source):
                fwd_copy(w, source).start()

    back_row = lax.broadcasted_iota(jnp.int32, (chunk * width, 1), 0)
    position = back_row & (capacity - 1)
    where_to = jnp.where(
        position < jnp.maximum(-lead, 0),
        WORK,
        jnp.where(position >= WORK - lead, WORK + 1, position + lead),
    )
    live = position < here
    target = (
        (where_to << (lc + lg))
        + (((back_row >> lcap) & (groups - 1)) << lc)
        + (back_row >> lw)
    )
    target = jnp.where(live, target, -1)
    home_row = lax.broadcasted_iota(jnp.int32, (chunk * width, SLOTS * block), 1)
    scatter = jnp.where(home_row == target, 1.0, 0.0).astype(BF16)

    for source in range(groups):
        for w, _, receives in sides:

            @pl.when(receives)
            def _(w=w, source=source):
                fwd_copy(w, source).wait_recv()

    for part in range(rows // chunk):
        span = pl.ds(part * chunk, chunk)
        parts = [home[:, span, lanes[w]] for w in both]
        parts.append(home_left[:, span, pl.ds(length - low, length)])
        parts.append(home_right[:, span, pl.ds(0, length)])
        parts = jnp.concatenate(
            [x.astype(F32).reshape(block, length).astype(BF16) for x in parts], axis=0
        )
        placed = dot(scatter, parts)
        kept = ens_ref[span].reshape(chunk * width, length).astype(F32)
        placed = jnp.where(live, placed, kept)
        out_ref[span] = placed.astype(BF16).reshape(chunk, width, length)

    for side, sends, _ in sides:

        @pl.when(sends)
        def _(side=side):
            obs_copy(side).wait_send()
            mrg_copy(side).wait_send()
            for source in range(groups):
                fwd_copy(side, source).wait_send()

    for step in range(1, groups):
        peer = lax.rem(me + step, groups)
        in_copy(peer, me).wait_send()
        out_copy(peer, me).wait_send()


def on_device(ensemble, departures, innovations, precision, obs_count, tile_counts):
    groups = lax.axis_size("member")
    tiles = lax.axis_size("tile")
    rows, width, length = ensemble.shape
    capacity, obs_rows, members = departures.shape
    vmem = pl.BlockSpec(memory_space=pltpu.VMEM)
    smem = pl.BlockSpec(memory_space=pltpu.SMEM)
    hbm = pl.BlockSpec(memory_space=pl.ANY)
    dma = pltpu.SemaphoreType.DMA
    return pl.pallas_call(
        functools.partial(kernel, tiles, groups),
        out_shape=pltpu.VMEM(ensemble.shape, BF16),
        in_specs=[smem, smem, hbm, hbm, hbm, hbm],
        out_specs=vmem,
        scratch_shapes=[
            pltpu.VMEM(ensemble.shape, BF16),
            pltpu.VMEM(departures.shape, BF16),
            pltpu.VMEM(innovations.shape, F32),
            pltpu.VMEM(precision.shape, F32),
            dma((4,)),
            pltpu.VMEM((groups, rows, WORK * length), BF16),
            pltpu.VMEM((2, groups, rows, length), BF16),
            pltpu.VMEM((2, groups, rows, length), BF16),
            pltpu.VMEM((2, obs_rows + 16, members), BF16),
            pltpu.VMEM((2, obs_rows + 16, members), BF16),
            pltpu.VMEM((groups, rows, WORK * length), BF16),
            pltpu.VMEM((groups, rows, WORK * length), BF16),
            pltpu.VMEM((groups, rows, WORK * length), BF16),
            pltpu.VMEM((groups, rows, WORK * length - length // 128 * 128), BF16),
            pltpu.VMEM((groups, rows, -(-length // 128) * 128), BF16),
            dma((2,)), dma((2,)), dma((2,)), dma((2,)),
            dma((groups,)), dma((groups,)),
            dma((groups,)), dma((groups,)),
            dma((WORK, groups)), dma((WORK, groups)),
        ],
        compiler_params=pltpu.CompilerParams(
            collective_id=0, has_side_effects=True, vmem_limit_bytes=56 * 1024 * 1024
        ),
    )(tile_counts, obs_count, ensemble, departures, innovations, precision)


def solution(mesh):
    placed = (
        P("member", "tile", None),
        P(("tile", "member"), None, None),
        P(("tile", "member"), None),
        P(("tile", "member"), None),
        P(("tile", "member")),
        P(),
    )
    return jax.shard_map(
        on_device, mesh=mesh, in_specs=placed, out_specs=P("member", "tile", None), check_vma=False
    )
```
